32 devices in a mesh: groups: 2 (over y), row: 4 (over z), col: 2 (over x), sub: 2 (over core).
Axes of the slice: x: 2, y: 2, z: 4, core: 2. Of those that a mesh axis runs over, the one named last changes fastest.
Arguments:
- latent: bfloat16 [512, 128, 320], P(('groups', 'row', 'sub'), 'col'), parts along dimension 0, may hold values from -6 to 6
- condition: bfloat16 [512, 4096], P(('groups', 'row', 'sub'), 'col'), parts along dimension 0, may hold values from -360 to 360
- conv_weight: bfloat16 [2, 3, 3, 320, 320], replicated, may hold values from -0.109375 to 0.109375
- conv_gain: float32 [2, 320], replicated, may hold values from 0.5 to 1.5
- attn_gain: float32 [2, 320], replicated, may hold values from 0.5 to 1.5
- q_weight: bfloat16 [2, 320, 320], replicated, may hold values from -0.3125 to 0.3125
- kv_weight: bfloat16 [4096, 1280], P('col'), may hold values from -0.09375 to 0.09375
- out_gain: float32 [2, 320], replicated, may hold values from 0.5 to 1.5
- out_weight: bfloat16 [2, 320, 320], replicated, may hold values from -0.3125 to 0.3125
Outputs:
- refined: float32 [512, 128, 320], P(('groups', 'row', 'sub'), 'col'), parts along dimension 0
The draws below stay inside these ranges and needn't reach their ends.
There are 2 independent parts, one for each index of `groups`. The reference program is written for one: setup_inputs(seed, part) draws one part's arguments, and reference() takes and returns one part's arrays. A program takes and returns all parts, laid end to end along the dimension named above; an argument that names none is the same for every part. Nothing has to cross between parts.
All inputs are finite; a program needn't handle non-finite values.
Results may differ from the reference program's by a relative error of at most 0.013.
The reference program's roundings to bfloat16 on the way count: a program that leaves them out, or rounds other values in their place, can miss the bound.
Values sent between devices are 32-bit elements; how exact they have to be, the bound alone decides.
A program may use at most 64 MiB of HBM per device.

```python
import math
import jax
import jax.numpy as jnp
from jax import lax

C = 320
HEADS = 5
TEXT = 4096
CTX = 256
BLOCKS = 2
HEAD = 64
NH = 256
NW = 128


def draw_condition(key, part):
    first_key = jax.random.fold_in(key, 0)
    return jnp.clip(jax.random.normal(first_key, (CTX, TEXT), jnp.float32), -6.0, 6.0).astype(jnp.bfloat16)


def block_scale(stream_key, dims, pieces, low, top_value):
    level = 1.0
    for dim, shards_of in pieces:
        steps = jax.random.uniform(jax.random.fold_in(jax.random.fold_in(stream_key, 6), dim), (shards_of,), jnp.float32, low / len(pieces), top_value / len(pieces))
        level = level * jnp.repeat(jnp.exp(steps), dims[dim] // shards_of).reshape((-1,) + (1,) * (len(dims) - 1 - dim))
    return level


def noise(own_key, shape, deviation, reach, pieces=(), dtype=jnp.bfloat16):
    loudness = block_scale(own_key, shape, pieces, -0.22, 0.18) if pieces else 1.0
    values = jax.random.normal(own_key, shape, jnp.float32) * deviation * loudness
    return jnp.minimum(jnp.maximum(values, -reach), reach).astype(dtype)


def setup_inputs(seed: int = 0, part: int = 0) -> dict:
    key_list = jax.random.split(jax.random.key(seed), 10)
    own_keys = jax.random.split(jax.random.fold_in(key_list[9], part), 10)
    latent = noise(own_keys[0], (NH, NW, C), 1.0, 6.0, ((0, 8), (1, 2)))
    condition = draw_condition(jax.random.fold_in(jax.random.fold_in(key_list[9], part), 71), part)
    conv_weight = noise(key_list[2], (BLOCKS, 3, 3, C, C), (9 * C) ** -0.5, 0.109375)
    conv_gain = jnp.clip(jax.random.uniform(key_list[3], (BLOCKS, C), jnp.float32, 0.5, 1.5), 0.5, 1.5)
    attn_gain = jnp.clip(jax.random.uniform(key_list[4], (BLOCKS, C), jnp.float32, 0.5, 1.5), 0.5, 1.5)
    q_weight = noise(key_list[5], (BLOCKS, C, C), C ** -0.5, 0.3125)
    kv_weight = noise(key_list[6], (TEXT, BLOCKS * 2 * C), TEXT ** -0.5, 0.09375, ((0, 2),))
    out_gain = jnp.clip(jax.random.uniform(key_list[7], (BLOCKS, C), jnp.float32, 0.5, 1.5), 0.5, 1.5)
    out_weight = noise(key_list[8], (BLOCKS, C, C), C ** -0.5, 0.3125)
    return {"latent": latent, "condition": condition, "conv_weight": conv_weight, "conv_gain": conv_gain, "attn_gain": attn_gain, "q_weight": q_weight, "kv_weight": kv_weight, "out_gain": out_gain, "out_weight": out_weight}


epsilon = 1e-06

def normed(values, scale_gain):
    values = values.astype(jnp.float32)
    return values * lax.rsqrt(lax.optimization_barrier(jnp.mean(values * values, axis=-1, keepdims=True)) + epsilon) * scale_gain

def convolve(active, tap_weights):
    all_rows, all_cols, channels = active.shape
    padded = jnp.pad(active, ((1, 1), (1, 1), (0, 0)))
    summed_taps = jnp.zeros((all_rows * all_cols, tap_weights.shape[-1]), jnp.float32)
    for shift_row in range(3):
        for shift_col in range(3):
            window = padded[shift_row:shift_row + all_rows, shift_col:shift_col + all_cols].reshape(-1, channels)
            summed_taps = summed_taps + jnp.dot(window, tap_weights[shift_row, shift_col], preferred_element_type=jnp.float32)
    return summed_taps

def attend(hidden, attn_scale, q_matrix, key_part, value_part, out_scale):
    cell_count = hidden.shape[0]
    normal_in = normed(hidden, attn_scale).astype(jnp.bfloat16)
    queries = jnp.dot(normal_in, q_matrix, preferred_element_type=jnp.float32)
    query_heads = queries.reshape(cell_count, HEADS, HEAD)
    key_heads = key_part.reshape(-1, HEADS, HEAD)
    value_heads = value_part.reshape(-1, HEADS, HEAD)
    scores = jnp.einsum('nhd,khd->hnk', query_heads, key_heads, precision=lax.Precision.HIGHEST) * (1.0 / math.sqrt(HEAD))
    row_max = lax.optimization_barrier(jnp.max(scores, axis=-1, keepdims=True))
    exponent = jnp.exp(scores - row_max)
    weights = exponent / lax.optimization_barrier(jnp.sum(exponent, axis=-1, keepdims=True))
    attended = jnp.einsum('hnk,khd->nhd', weights, value_heads, precision=lax.Precision.HIGHEST).reshape(cell_count, HEADS * HEAD)
    return normed(attended, out_scale).astype(jnp.bfloat16)

def reference(latent, condition, conv_weight, conv_gain, attn_gain, q_weight, kv_weight, out_gain, out_weight):
    projected = jnp.dot(condition, kv_weight, preferred_element_type=jnp.float32)
    current = latent.astype(jnp.float32)
    for block_index in range(BLOCKS):
        key_part = projected[:, 2 * C * block_index:2 * C * block_index + C]
        value_part = projected[:, 2 * C * block_index + C:2 * C * (block_index + 1)]
        active = jax.nn.silu(normed(current, conv_gain[block_index])).astype(jnp.bfloat16)
        hidden = current.reshape(-1, C) + convolve(active, conv_weight[block_index])
        grid_hidden = hidden.reshape(NH, NW, C)
        attn_out = lax.map(lambda image_row: attend(image_row, attn_gain[block_index], q_weight[block_index], key_part, value_part, out_gain[block_index]), grid_hidden)
        update = jnp.dot(attn_out.reshape(-1, C), out_weight[block_index], preferred_element_type=jnp.float32)
        current = (hidden + update).reshape(NH, NW, C)
    return current
```

```python
import functools

import jax
import jax.numpy as jnp
from jax import lax
from jax.experimental import pallas as pl
from jax.experimental.pallas import tpu as pltpu
from jax.sharding import PartitionSpec as P

HEADS = 5
BLOCKS = 2
HEAD = 64
C = HEADS * HEAD
TAPS = 3 * C
epsilon = 1e-06
BF = jnp.bfloat16
F32 = jnp.float32


def with_halo(cells, sides, width):
    for axis, dim in sides:
        count = lax.axis_size(axis)
        ends = count - 1
        head = lax.slice_in_dim(cells, 0, width, axis=dim)
        tail = lax.slice_in_dim(cells, cells.shape[dim] - width, cells.shape[dim], axis=dim)
        cells = jnp.concatenate(
            [
                lax.ppermute(tail, axis, [(i, (i + 1) % count) for i in range(ends)]),
                cells,
                lax.ppermute(head, axis, [((i + 1) % count, i) for i in range(ends)]),
            ],
            axis=dim,
        )
    return cells


def normed(values, gain):
    mean = jnp.sum(values * values, axis=-1, keepdims=True) * (1.0 / C)
    return values * lax.rsqrt(mean + epsilon) * gain


def hi_lo(values):
    high = values.astype(BF)
    low = (values - high.astype(F32)).astype(BF)
    return high, low


def blocks_kernel(
    rows, cols, wide,
    bounds, xpad, projected, conv_w, conv_gain, attn_gain, q_w, out_gain, out_w,
    out, acat, x1, shift, kcat, vcat, q_dup,
):
    tokens = projected.shape[0]

    def prepare(b):
        base = 2 * C * b
        ones = jnp.ones((tokens, HEAD), BF)
        zeros = jnp.zeros((tokens, HEAD), BF)
        for h in range(HEADS):
            high, low = hi_lo(projected[:, base + HEAD * h : base + HEAD * (h + 1)])
            kcat[h] = jnp.concatenate([high, high, low, low], axis=-1)
            v = projected[:, base + C + HEAD * h : base + C + HEAD * (h + 1)].astype(BF)
            parts = [v, zeros, ones, zeros] if h % 2 == 0 else [zeros, v, zeros, ones]
            vcat[h] = jnp.concatenate(parts, axis=-1)
            w = q_w[b, :, HEAD * h : HEAD * (h + 1)]
            q_dup[:, 2 * HEAD * h : 2 * HEAD * (h + 1)] = jnp.concatenate([w, w], axis=-1)

    def activate(b, source, count, win, wout, masked):
        gain = conv_gain[b : b + 1, :]

        def one(r, carry):
            value = normed(source[r], gain)
            value = value / (1.0 + jnp.exp(-value))
            if masked:
                at = lax.broadcasted_iota(jnp.int32, (win, 1), 0)
                row_ok = jnp.logical_and(r >= bounds[0], r < bounds[1])
                ok = jnp.logical_and(at >= bounds[2], at < bounds[3])
                value = jnp.where(jnp.logical_and(ok, row_ok), value, 0.0)
            shift[0:win, :] = value
            acat[r, 0:wout, :] = jnp.concatenate(
                [shift[j : j + wout, :].astype(BF) for j in range(3)], axis=-1
            )
            return carry

        lax.fori_loop(0, count, one, 0)

    def chunk(b, source, r0, n, wout):
        cells = n * wout
        total = source[pl.ds(r0 + 1, n), 1 : 1 + wout, :].reshape(cells, C)
        for i in range(3):
            window = acat[pl.ds(r0 + i, n), 0:wout, :].reshape(cells, TAPS)
            total = total + jnp.dot(window, conv_w[b, i], preferred_element_type=F32)
        hidden = total
        normal = normed(hidden, attn_gain[b : b + 1, :]).astype(BF)
        query = jnp.dot(normal, q_dup[...], preferred_element_type=F32) * 0.125
        lane = lax.broadcasted_iota(jnp.int32, (1, 2 * HEAD), 1)
        pieces = []
        for g in range(3):
            both = None
            for h in range(2 * g, min(2 * g + 2, HEADS)):
                qh = query[:, 2 * HEAD * h : 2 * HEAD * (h + 1)]
                high = qh.astype(BF).astype(F32)
                t = jnp.where(lane < HEAD, high, qh - high).astype(BF)
                scores = lax.dot_general(
                    jnp.concatenate([t, t], axis=-1), kcat[h],
                    (((1,), (1,)), ((), ())), preferred_element_type=F32,
                )
                p = jnp.exp(scores - jnp.max(scores, axis=-1, keepdims=True)).astype(BF)
                o = jnp.dot(p, vcat[h], preferred_element_type=F32)
                both = o if both is None else both + o
            if g == 2:
                pieces.append(both[:, :HEAD] / both[:, 2 * HEAD : 3 * HEAD])
            else:
                pieces.append(both[:, : 2 * HEAD] / both[:, 2 * HEAD :])
        attended = jnp.concatenate(pieces, axis=-1)
        mixed = normed(attended, out_gain[b : b + 1, :]).astype(BF)
        update = jnp.dot(mixed, out_w[b], preferred_element_type=F32)
        return (hidden + update).reshape(n, wout, C)

    prepare(0)
    activate(0, xpad, rows + 4, wide + 8, wide, False)
    n0 = 7
    steps0 = -(-(rows + 2) // n0)

    def step0(k, carry):
        r0 = jnp.minimum(k * n0, rows + 2 - n0)
        x1[pl.ds(r0, n0)] = chunk(0, xpad, r0, n0, wide)
        return carry

    lax.fori_loop(0, steps0, step0, 0)
    prepare(1)
    activate(1, x1, rows + 2, wide, cols, True)
    n1 = 8

    def step1(k, carry):
        r0 = k * n1
        out[pl.ds(r0, n1)] = chunk(1, x1, r0, n1, cols)
        return carry

    lax.fori_loop(0, rows // n1, step1, 0)


def shards(
    latent, condition, conv_weight, conv_gain, attn_gain, q_weight, kv_weight, out_gain, out_weight
):
    rows, cols, _ = latent.shape
    wide = cols + 8
    partial_value = jnp.dot(condition, kv_weight, preferred_element_type=F32)
    summed = lax.psum(partial_value, "col")
    projected = lax.all_gather(summed, ("row", "sub"), axis=0, tiled=True)
    tokens = projected.shape[0]
    padded = with_halo(latent.astype(F32), ((("row", "sub"), 0), ("col", 1)), 2)
    padded = jnp.pad(padded, ((0, 0), (0, wide + 8 - cols - 4), (0, 0)))
    subs, col_count = lax.axis_size("sub"), lax.axis_size("col")
    tile = lax.axis_index("row") * subs + lax.axis_index("sub")
    last = lax.axis_size("row") * subs - 1
    col = lax.axis_index("col")
    bounds = jnp.stack([
        jnp.where(tile == 0, 1, 0),
        jnp.where(tile == last, rows + 1, rows + 2),
        jnp.where(col == 0, 1, 0),
        jnp.where(col == col_count - 1, cols + 1, cols + 2),
    ]).astype(jnp.int32)
    vmem = pl.BlockSpec(memory_space=pltpu.VMEM)
    return pl.pallas_call(
        functools.partial(blocks_kernel, rows, cols, wide),
        out_shape=jax.ShapeDtypeStruct((rows, cols, C), F32),
        in_specs=[pl.BlockSpec(memory_space=pltpu.SMEM)] + [vmem] * 8,
        out_specs=vmem,
        scratch_shapes=[
            pltpu.VMEM((rows + 4, wide, TAPS), BF),
            pltpu.VMEM((rows + 2, wide, C), F32),
            pltpu.VMEM((wide + 8, C), F32),
            pltpu.VMEM((HEADS, tokens, 4 * HEAD), BF),
            pltpu.VMEM((HEADS, tokens, 4 * HEAD), BF),
            pltpu.VMEM((C, 2 * C), BF),
        ],
        compiler_params=pltpu.CompilerParams(vmem_limit_bytes=56 * 1024 * 1024),
    )(
        bounds, padded, projected, conv_weight.reshape(BLOCKS, 3, TAPS, C),
        conv_gain, attn_gain, q_weight, out_gain, out_weight,
    )


def solution(mesh):
    placed = (
        P(("groups", "row", "sub"), "col", None),
        P(("groups", "row", "sub"), "col"),
        P(),
        P(),
        P(),
        P(),
        P("col", None),
        P(),
        P(),
    )
    return jax.shard_map(
        shards,
        mesh=mesh,
        in_specs=placed,
        out_specs=P(("groups", "row", "sub"), "col", None),
        check_vma=False,
    )
```
